512 devices in a mesh: tm: 16 (over z_hi, x), band: 32 (over z_lo, y, core).
Axes of the slice: x: 4, y: 8, z: 8 (z_hi: 4, z_lo: 2; z = z_hi * 2 + z_lo), core: 2. Of those that a mesh axis runs over, the one named last changes fastest.
Arguments:
- increments: float32 [16, 4, 2, 1024, 1024], P('tm', None, None, 'band'), may hold values from -6 to 6
- velocity: float32 [16, 2, 1024, 1024], P('tm', None, 'band'), may hold values from -0.4 to 0.4
- diffusivity: float32 [4, 2], replicated, may hold values from 0.03 to 0.22
- scaling: float32 [4, 2, 1024, 1024], P(None, None, 'band'), may hold values from 0.3 to 3
- correlation: float32 [1024, 1024], P('band'), may hold values from -0.2 to 0.5
Outputs:
- weighted_defects: float32 [16, 4, 2, 1024, 1024], P('tm', None, None, 'band')
The draws below stay inside these ranges and needn't reach their ends.
All inputs are finite; a program needn't handle non-finite values.
Results may differ from the reference program's by a relative error of at most 0.000094.
Values sent between devices are 32-bit elements; how exact they have to be, the bound alone decides.
No kernel may reach another device: no remote copies, remote signals or barrier semaphores. Data moves between devices by JAX's collectives and lax.ppermute only.
A program may use at most 64 MiB of HBM per device.

```python
import math
import jax
import jax.numpy as jnp
from jax import lax

GRID = 1024
FIELDS = 4
LEVELS = 2
STEPS = 4
WINDOWS = 16


def draw_correlation(key, part):
    index_all = jnp.arange(GRID)
    apart = jnp.abs(index_all[:, None] - index_all[None, :]).astype(jnp.float32)
    first_key, second_key = jax.random.split(jax.random.fold_in(key, 11))
    factor = jax.random.uniform(first_key, (GRID, GRID), jnp.float32, 0.5, 1.5)
    noise = jnp.clip(jax.random.normal(second_key, (GRID, GRID), jnp.float32), -5.0, 5.0) * 0.05
    reach = GRID // 16
    matrix = jnp.eye(GRID, dtype=jnp.float32) + 0.6 * jnp.exp(-apart / reach) * factor + noise
    return 0.2 * matrix


def levels(stream_key, shape, shards, smallest, largest):
    level, own = 1.0, jax.random.fold_in(stream_key, 6)
    for position, blocks in shards:
        heights = jnp.exp(jax.random.uniform(jax.random.fold_in(own, position), (blocks,), jnp.float32, smallest / len(shards), largest / len(shards)))
        level = level * jnp.repeat(heights, shape[position] // blocks).reshape([-1 if axis == position else 1 for axis in range(len(shape))])
    return level


def normal_values(own_key, shape, deviation, bound, shards=(), held_as=jnp.bfloat16):
    values = deviation * jax.random.normal(own_key, shape, jnp.float32)
    if shards:
        values = values * levels(own_key, shape, shards, -0.22, 0.18)
    return jnp.clip(values, -bound, bound).astype(held_as)


def setup_inputs(seed: int = 0) -> dict:
    key_list = jax.random.split(jax.random.key(seed), 6)
    return {
        "increments": normal_values(key_list[0], (WINDOWS, FIELDS, LEVELS, GRID, GRID), 1.0, 6.0, ((0, 16), (3, 32)), jnp.float32),
        "velocity": jnp.clip(jax.random.uniform(key_list[1], (WINDOWS, 2, GRID, GRID), jnp.float32, -0.4, 0.4) * levels(key_list[1], (WINDOWS, 2, GRID, GRID), ((0, 16), (2, 32)), -0.4, 0.0), -0.4, 0.4),
        "diffusivity": jnp.clip(jnp.exp(jax.random.uniform(key_list[2], (FIELDS, LEVELS), jnp.float32, math.log(0.03), math.log(0.22))), 0.03, 0.22),
        "scaling": jnp.clip(jnp.exp(math.log(3.0) - 2.3025851 * jax.random.uniform(key_list[3], (FIELDS, LEVELS, GRID, GRID), jnp.float32) ** levels(key_list[3], (FIELDS, LEVELS, GRID, GRID), ((2, 32),), -0.2, 0.2)), 0.3, 3.0),
        "correlation": draw_correlation(jax.random.fold_in(key_list[5], 71), 0),
    }


def advance(current, east_speed, north_speed, diffuse):
    padded = jnp.pad(current, ((0, 0), (1, 1), (0, 0)))
    upper = padded[:, 2:]
    lower = padded[:, :-2]
    eastern = jnp.roll(current, -1, 2)
    western = jnp.roll(current, 1, 2)
    return (current - 0.5 * east_speed * (eastern - western) - 0.5 * north_speed * (upper - lower)
            + diffuse * (upper + lower + eastern + western - 4.0 * current))


def propagate(initial, speeds, diffuse):
    current = initial
    for section_num in range(STEPS):
        current = advance(current, speeds[0], speeds[1], diffuse)
    return current


def reference(increments, velocity, diffusivity, scaling, correlation):
    channels = FIELDS * LEVELS
    diffuse = diffusivity.reshape(channels, 1, 1)
    sigma = scaling.reshape(channels, GRID, GRID)

    def run_window(pair):
        return propagate(pair[0].reshape(channels, GRID, GRID), pair[1], diffuse)

    ends = lax.map(run_window, (increments, velocity))
    previous = jnp.concatenate([jnp.zeros_like(ends[:1]), ends[:-1]], axis=0)

    def finish(pair):
        defect = pair[0].reshape(channels, GRID, GRID) - pair[1]
        scaled = sigma * defect
        along = jnp.einsum('fyj,ij->fyi', scaled, correlation, precision=lax.Precision.HIGHEST)
        both = jnp.einsum('iy,fyx->fix', correlation, along, precision=lax.Precision.HIGHEST)
        return (sigma * both).reshape(FIELDS, LEVELS, GRID, GRID)

    return lax.map(finish, (increments, previous))
```

```python
import jax
import jax.numpy as jnp
from jax import lax
from jax.experimental import pallas as pl
from jax.experimental.pallas import tpu as pltpu
from jax.sharding import PartitionSpec as P

FIELDS = 4
LEVELS = 2
STEPS = 4
CH = FIELDS * LEVELS
ROWS = 32
GRID = 1024
BANDS = 32
QUARTERS = BANDS // CH
COLS = GRID // QUARTERS
F32 = jnp.float32
BF16 = jnp.bfloat16
VMEM_LIMIT = 48 << 20


def params(**kw):
    return pltpu.CompilerParams(vmem_limit_bytes=VMEM_LIMIT, **kw)


def pack_kernel(x_top, x_bot, v_top, v_bot, lo_ref, hi_ref):
    row = lax.broadcasted_iota(jnp.int32, (8, GRID), 0)
    for k in range(CH // 2 + 1):
        if k < CH // 2:
            ta, tb, ba, bb = x_top[2 * k], x_top[2 * k + 1], x_bot[2 * k], x_bot[2 * k + 1]
        else:
            ta, tb, ba, bb = v_top[0], v_top[1], v_bot[0], v_bot[1]
        lo_ref[k] = jnp.where(row < 4, ta, pltpu.roll(tb, 4, 0))
        hi_ref[k] = jnp.where(row < 4, pltpu.roll(ba, 4, 0), bb)


def pack_edges(x, v):
    tiles = CH // 2 + 1
    shape = jax.ShapeDtypeStruct((tiles, 8, GRID), F32)
    last = ROWS // 8 - 1
    return pl.pallas_call(
        pack_kernel,
        grid=(1,),
        out_shape=(shape, shape),
        in_specs=[
            pl.BlockSpec((CH, 8, GRID), lambda i: (0, 0, 0)),
            pl.BlockSpec((CH, 8, GRID), lambda i: (0, last, 0)),
            pl.BlockSpec((2, 8, GRID), lambda i: (0, 0, 0)),
            pl.BlockSpec((2, 8, GRID), lambda i: (0, last, 0)),
        ],
        out_specs=(pl.BlockSpec((tiles, 8, GRID), lambda i: (0, 0, 0)),) * 2,
        compiler_params=params(),
        name="pack_edges",
    )(x, x, v, v)


def stencil_kernel(k_ref, m_ref, x_ref, v_ref, before_ref, after_ref, o_ref, buf, vel):
    c = pl.program_id(0)

    @pl.when(c == 0)
    def _():
        zeros = jnp.zeros((8, GRID), F32)
        for s in range(2):
            buf[s, 0:8] = zeros
            buf[s, 56:64] = zeros
        for d in range(2):
            top, bot = before_ref[CH // 2], after_ref[CH // 2]
            vel[d, 0:8] = 0.5 * (pltpu.roll(top, 4, 0) if d == 0 else top)
            vel[d, 8:40] = 0.5 * v_ref[d]
            vel[d, 40:48] = 0.5 * (bot if d == 0 else pltpu.roll(bot, 4, 0))

    half = c // 2
    odd = c % 2
    top, bot = before_ref[half], after_ref[half]
    buf[0, 8:16] = jnp.where(odd == 0, pltpu.roll(top, 4, 0), top)
    buf[0, 16:48] = x_ref[0]
    buf[0, 48:56] = jnp.where(odd == 0, bot, pltpu.roll(bot, 4, 0))
    k = k_ref[c]
    for s in range(STEPS):
        src, dst = s % 2, (s + 1) % 2
        last = s == STEPS - 1
        for t in range(1, 5) if last else range(6):
            r = 8 + 8 * t
            kk = k * m_ref[0] if t == 0 else k * m_ref[1] if t == 5 else k
            x = buf[src, r : r + 8]
            up = buf[src, r + 1 : r + 9]
            lo = buf[src, r - 1 : r + 7]
            e = pltpu.roll(x, GRID - 1, 1)
            w = pltpu.roll(x, 1, 1)
            hu = vel[0, 8 * t : 8 * t + 8]
            hv = vel[1, 8 * t : 8 * t + 8]
            y = x - hu * (e - w) - hv * (up - lo) + kk * (up + lo + e + w - 4.0 * x)
            if last:
                o_ref[0, r - 16 : r - 8] = y
            else:
                buf[dst, r : r + 8] = y


def propagate(x, v, before, after, diffuse, inside):
    tiles = CH // 2 + 1
    whole = pl.BlockSpec((tiles, 8, GRID), lambda c: (0, 0, 0))
    smem = pl.BlockSpec(memory_space=pltpu.SMEM)
    return pl.pallas_call(
        stencil_kernel,
        grid=(CH,),
        out_shape=jax.ShapeDtypeStruct((CH, ROWS, GRID), F32),
        in_specs=[
            smem,
            smem,
            pl.BlockSpec((1, ROWS, GRID), lambda c: (c, 0, 0)),
            pl.BlockSpec((2, ROWS, GRID), lambda c: (0, 0, 0)),
            whole,
            whole,
        ],
        out_specs=pl.BlockSpec((1, ROWS, GRID), lambda c: (c, 0, 0)),
        scratch_shapes=[pltpu.VMEM((2, 64, GRID), F32), pltpu.VMEM((2, 48, GRID), F32)],
        compiler_params=params(),
        name="propagate",
    )(diffuse, inside, x, v, before, after)


def combine_kernel(x_ref, a_ref, s_ref, o_ref):
    y = s_ref[0] * (x_ref[0] - a_ref[0])
    for q in range(QUARTERS):
        o_ref[q] = y[:, q * COLS : (q + 1) * COLS]


def combine(x, arrived, sigma):
    spec = pl.BlockSpec((1, ROWS, GRID), lambda c: (c, 0, 0))
    return pl.pallas_call(
        combine_kernel,
        grid=(CH,),
        out_shape=jax.ShapeDtypeStruct((BANDS, ROWS, COLS), F32),
        in_specs=[spec] * 3,
        out_specs=pl.BlockSpec((QUARTERS, ROWS, COLS), lambda c: (c, 0, 0)),
        compiler_params=params(),
        name="combine",
    )(x, arrived, sigma)


def halves(x):
    hi = x.astype(BF16)
    return hi, (x - hi.astype(F32)).astype(BF16)


def split_kernel(c_ref, hi_ref, lo_ref):
    hi_ref[...], lo_ref[...] = halves(c_ref[...])


def split(c):
    spec = pl.BlockSpec((256, GRID), lambda i: (i, 0))
    shape = jax.ShapeDtypeStruct((GRID, GRID), BF16)
    return pl.pallas_call(
        split_kernel,
        grid=(GRID // 256,),
        out_shape=(shape, shape),
        in_specs=[spec],
        out_specs=(spec, spec),
        compiler_params=params(),
        name="split",
    )(c)


def rows_kernel(hi_ref, lo_ref, x_ref, o_ref, xh, xl):
    @pl.when(pl.program_id(0) == 0)
    def _():
        xh[...], xl[...] = halves(x_ref[...])

    dot = lambda a, b: jnp.dot(a, b, preferred_element_type=F32)
    o_ref[...] = dot(hi_ref[...], xl[...]) + dot(lo_ref[...], xh[...]) + dot(hi_ref[...], xh[...])


def mix_rows(hi, lo, x):
    spec = pl.BlockSpec((256, GRID), lambda i: (i, 0))
    return pl.pallas_call(
        rows_kernel,
        grid=(GRID // 256,),
        out_shape=jax.ShapeDtypeStruct((GRID, COLS), F32),
        in_specs=[spec, spec, pl.BlockSpec((GRID, COLS), lambda i: (0, 0))],
        out_specs=pl.BlockSpec((256, COLS), lambda i: (i, 0)),
        scratch_shapes=[pltpu.VMEM((GRID, COLS), BF16)] * 2,
        compiler_params=params(),
        name="mix_rows",
    )(hi, lo, x)


def columns_kernel(hi_ref, lo_ref, r_ref, s_ref, o_ref, rh, rl):
    @pl.when(pl.program_id(0) == 0)
    def _():
        for q in range(QUARTERS):
            h, l = halves(r_ref[:, q].reshape(CH * ROWS, COLS))
            rh[:, q * COLS : (q + 1) * COLS] = h
            rl[:, q * COLS : (q + 1) * COLS] = l

    dot = lambda a, b: lax.dot_general(a, b, (((1,), (1,)), ((), ())), preferred_element_type=F32)
    y = dot(rl[...], hi_ref[...]) + dot(rh[...], lo_ref[...]) + dot(rh[...], hi_ref[...])
    o_ref[...] = s_ref[...] * y.reshape(CH, ROWS, 256)


def mix_columns(hi, lo, r, sigma):
    spec = pl.BlockSpec((256, GRID), lambda i: (i, 0))
    out = pl.BlockSpec((CH, ROWS, 256), lambda i: (0, 0, i))
    return pl.pallas_call(
        columns_kernel,
        grid=(GRID // 256,),
        out_shape=jax.ShapeDtypeStruct((CH, ROWS, GRID), F32),
        in_specs=[spec, spec, pl.BlockSpec((CH, QUARTERS, ROWS, COLS), lambda i: (0, 0, 0, 0)), out],
        out_specs=out,
        scratch_shapes=[pltpu.VMEM((CH * ROWS, GRID), BF16)] * 2,
        compiler_params=params(),
        name="mix_columns",
    )(hi, lo, r.reshape(CH, QUARTERS, ROWS, COLS), sigma)


def local(increments, velocity, diffusivity, scaling, correlation):
    x = increments.reshape(CH, ROWS, GRID)
    v = velocity[0]
    sigma = scaling.reshape(CH, ROWS, GRID)
    full = lax.all_gather(correlation, "band", axis=0, tiled=True)
    up = [(i, i + 1) for i in range(BANDS - 1)]
    down = [(j, i) for i, j in up]
    lo_edge, hi_edge = pack_edges(x, v)
    before = lax.ppermute(hi_edge, "band", up)
    after = lax.ppermute(lo_edge, "band", down)
    band = lax.axis_index("band")
    inside = jnp.stack([band > 0, band < BANDS - 1]).astype(F32)
    ends = propagate(x, v, before, after, diffusivity.reshape(CH), inside)
    windows = lax.axis_size("tm")
    arrived = lax.ppermute(ends, "tm", [(i, i + 1) for i in range(windows - 1)])
    sent = combine(x, arrived, sigma)
    mine = lax.all_to_all(sent, "band", 0, 0, tiled=True).reshape(GRID, COLS)
    hi, lo = split(full)
    mixed = mix_rows(hi, lo, mine).reshape(BANDS, ROWS, COLS)
    back = lax.all_to_all(mixed, "band", 0, 0, tiled=True)
    return mix_columns(hi, lo, back, sigma).reshape(1, FIELDS, LEVELS, ROWS, GRID)


def solution(mesh):
    return jax.shard_map(
        local,
        mesh=mesh,
        in_specs=(
            P("tm", None, None, "band", None),
            P("tm", None, "band", None),
            P(),
            P(None, None, "band", None),
            P("band", None),
        ),
        out_specs=P("tm", None, None, "band", None),
        check_vma=False,
    )
```

```python
import functools

import jax
import jax.numpy as jnp
from jax import lax
from jax.experimental import pallas as pl
from jax.experimental.pallas import tpu as pltpu
from jax.sharding import PartitionSpec as P


FIELDS = 4
LEVELS = 2
STEPS = 4
CH = FIELDS * LEVELS
ROWS = 32
GRID = 1024
BANDS = 32
QUARTERS = BANDS // CH
COLS = GRID // QUARTERS
PLANES = 4
F32 = jnp.float32
BF16 = jnp.bfloat16


def in_hbm(*arrays):
    return [pltpu.with_memory_space_constraint(a, pltpu.HBM) for a in arrays]


def start_all(pairs, sem):
    copies = [pltpu.make_async_copy(src, dst, sem.at[i]) for i, (src, dst) in enumerate(pairs)]
    for copy in copies:
        copy.start()
    return copies


def params(mib):
    return pltpu.CompilerParams(vmem_limit_bytes=mib << 20)


VMEM = pl.BlockSpec(memory_space=pltpu.VMEM)
SMEM = pl.BlockSpec(memory_space=pltpu.SMEM)
HBM = pl.BlockSpec(memory_space=pltpu.HBM)
EDGE = jax.ShapeDtypeStruct((CH // 2 + 1, 8, GRID), F32)


def pack_kernel(x_hbm, v_hbm, lo_ref, hi_ref, xe, ve, sem):
    pairs = [
        (src.at[:, at : at + 8], dst.at[j]) for src, dst in ((x_hbm, xe), (v_hbm, ve)) for j, at in enumerate((0, ROWS - 8))
    ]
    for copy in start_all(pairs, sem):
        copy.wait()
    row = lax.broadcasted_iota(jnp.int32, (8, GRID), 0)
    for k in range(CH // 2 + 1):
        ref, at = (xe, 2 * k) if k < CH // 2 else (ve, 0)
        lo_ref[k] = jnp.where(row < 4, ref[0, at], pltpu.roll(ref[0, at + 1], 4, 0))
        hi_ref[k] = jnp.where(row < 4, pltpu.roll(ref[1, at], 4, 0), ref[1, at + 1])


def pack_edges(x, v):
    return pl.pallas_call(
        pack_kernel,
        out_shape=(EDGE, EDGE),
        in_specs=[HBM, HBM],
        out_specs=(VMEM, VMEM),
        scratch_shapes=[
            pltpu.VMEM((2, CH, 8, GRID), F32),
            pltpu.VMEM((2, 2, 8, GRID), F32),
            pltpu.SemaphoreType.DMA((4,)),
        ],
        compiler_params=params(3),
        name="pack_edges",
    )(*in_hbm(x, v))


def stencil_kernel(base, k_ref, band_ref, x_hbm, v_hbm, before_hbm, after_hbm, o_ref, first, second, buf, vel, x_ref, v_ref, *edges):
    before_ref, after_ref, sem = edges
    pairs = ((before_hbm, before_ref), (after_hbm, after_ref), (v_hbm, v_ref), (x_hbm.at[base : base + CH // 2], x_ref))
    for copy in start_all(pairs, sem):
        copy.wait()
    row = lax.broadcasted_iota(jnp.int32, (8, GRID), 0)

    def edge(above, below, odd):
        swap = lambda t: pltpu.roll(t, 4, 0)
        pick = lambda a, b: jnp.where(row < 4, b, a)
        return pick(above, swap(below)) if odd else pick(swap(above), below)

    for d in range(2):
        vel[d, 0:8] = 0.5 * edge(before_ref[CH // 2], after_ref[CH // 2], d)
        vel[d, 8:40] = 0.5 * v_ref[d]
    band = band_ref[0]
    within = jnp.where(row < 4, (band < BANDS - 1).astype(F32), (band > 0).astype(F32))

    def field(pair, odd):
        c = 2 * pair + odd
        pairs_ref = (first, second)[pair]
        k = k_ref[base + c]
        outer = k * within
        fringe = edge(before_ref[base // 2 + pair], after_ref[base // 2 + pair], odd)
        buf[0, 0:8] = fringe
        buf[0, 8:40] = x_ref[c]
        buf[0, 40:48] = fringe
        for s in range(STEPS):
            src, dst = s % 2, (s + 1) % 2
            last = s == STEPS - 1
            for t in range(1 if last else 0, 5):
                r = 8 * t
                kk = k if t else outer
                x = buf[src, r : r + 8]
                up = buf[src, r + 1 : r + 9]
                lo = buf[src, r - 1 : r + 7] if t else buf[src, 39:47]
                e = pltpu.roll(x, GRID - 1, 1)
                w = pltpu.roll(x, 1, 1)
                y = x - vel[0, r : r + 8] * (e - w) - vel[1, r : r + 8] * (up - lo)
                y = y + kk * (up + lo + e + w - 4.0 * x)
                if last:
                    o_ref[c, r - 8 : r] = y
                    pairs_ref[odd, r - 8 : r] = y
                else:
                    buf[dst, r : r + 8] = y
                    if t == 0:
                        buf[dst, 40:48] = y

    for pair in range(2):
        field(pair, 0)
        field(pair, 1)


def propagate(base, x, v, before, after, diffuse, band):
    return pl.pallas_call(
        functools.partial(stencil_kernel, base),
        out_shape=tuple(jax.ShapeDtypeStruct((n, ROWS, GRID), F32) for n in (4, 2, 2)),
        in_specs=[SMEM, SMEM, HBM, HBM, HBM, HBM],
        out_specs=(VMEM, VMEM, VMEM),
        scratch_shapes=[
            pltpu.VMEM((2, 48, GRID), F32),
            pltpu.VMEM((2, 40, GRID), F32),
            pltpu.VMEM((CH // 2, ROWS, GRID), F32),
            pltpu.VMEM((2, ROWS, GRID), F32),
            pltpu.VMEM(EDGE.shape, F32),
            pltpu.VMEM(EDGE.shape, F32),
            pltpu.SemaphoreType.DMA((4,)),
        ],
        compiler_params=params(4),
        name="propagate",
    )(diffuse, band, *in_hbm(x, v, before, after))


def combine_kernel(x_ref, along0, along1, p0, p1, p2, p3, s_ref, o_hbm, buf, sem):
    half = CH // 2
    copies = []
    for c in range(CH):
        arrived = (along0 if c < half else along1)[c % half] + (p0, p1, p2, p3)[c // 2][c % 2]
        y = s_ref[c] * (x_ref[c] - arrived)
        at = slice(c * QUARTERS, (c + 1) * QUARTERS)
        for q in range(QUARTERS):
            buf[c * QUARTERS + q] = y[:, q * COLS : (q + 1) * COLS]
        copy = pltpu.make_async_copy(buf.at[at], o_hbm.at[at], sem.at[c])
        copy.start()
        copies.append(copy)
    for copy in copies:
        copy.wait()


def combine(x, arrived, sigma):
    return pl.pallas_call(
        combine_kernel,
        out_shape=jax.ShapeDtypeStruct((BANDS, ROWS, COLS), F32),
        in_specs=[VMEM] * 8,
        out_specs=HBM,
        scratch_shapes=[pltpu.VMEM((BANDS, ROWS, COLS), F32), pltpu.SemaphoreType.DMA((CH,))],
        compiler_params=params(3),
        name="combine",
    )(x, *arrived, sigma)


def halves(x):
    hi = x.astype(BF16)
    return hi, (x - hi.astype(F32)).astype(BF16)


def deal_kernel(c_hbm, o_ref, c_ref, sem):
    for copy in start_all(((c_hbm, c_ref),), sem):
        copy.wait()
    for d in range(BANDS):
        at = quarter_of(d) * COLS
        o_ref[d] = c_ref[:, at : at + COLS]


def quarter_of(band):
    return (band & 1) * 2 + band // (BANDS // 2)


def deal(c):
    return pl.pallas_call(
        deal_kernel,
        out_shape=jax.ShapeDtypeStruct((BANDS, ROWS, COLS), F32),
        in_specs=[HBM],
        out_specs=VMEM,
        scratch_shapes=[pltpu.VMEM((ROWS, GRID), F32), pltpu.SemaphoreType.DMA((1,))],
        compiler_params=params(2),
        name="deal",
    )(*in_hbm(c))


def rows_kernel(quarter_ref, own, beside, across, both, x_ref, o_ref, hi_ref, lo_ref, xh, xl):
    @pl.when(pl.program_id(0) == 0)
    def _():
        xh[...], xl[...] = halves(x_ref[...].reshape(GRID, COLS))

    for flip, ref in ((0, own), (1, beside), (2, across), (3, both)):
        at = pl.ds(pl.multiple_of((quarter_ref[0] ^ flip) * COLS, COLS), COLS)
        hi_ref[:, at], lo_ref[:, at] = halves(ref[...].reshape(256, COLS))
    dot = lambda a, b: jnp.dot(a, b, preferred_element_type=F32)
    y = dot(hi_ref[...], xl[...]) + dot(lo_ref[...], xh[...]) + dot(hi_ref[...], xh[...])
    o_ref[...] = y.reshape(8, ROWS, COLS)


def mix_rows(quarter, blocks, x):
    block = pl.BlockSpec((8, ROWS, COLS), lambda i: (i, 0, 0))
    whole = pl.BlockSpec((256, GRID), lambda i: (i, 0))
    shape = jax.ShapeDtypeStruct((GRID, GRID), BF16)
    return pl.pallas_call(
        rows_kernel,
        grid=(GRID // 256,),
        out_shape=(jax.ShapeDtypeStruct((BANDS, ROWS, COLS), F32), shape, shape),
        in_specs=[SMEM] + [block] * QUARTERS + [pl.BlockSpec((BANDS, ROWS, COLS), lambda i: (0, 0, 0))],
        out_specs=(block, whole, whole),
        scratch_shapes=[pltpu.VMEM((GRID, COLS), BF16)] * 2,
        compiler_params=params(12),
        name="mix_rows",
    )(quarter, *blocks, x)


def columns_kernel(hi_ref, lo_ref, r_ref, s_ref, o_ref, rh, rl):
    for c in range(CH):
        for q in range(QUARTERS):
            at = slice(c * ROWS, (c + 1) * ROWS), slice(q * COLS, (q + 1) * COLS)
            rh[at], rl[at] = halves(r_ref[c * QUARTERS + q])

    dot = lambda a, b: lax.dot_general(a, b, (((1,), (1,)), ((), ())), preferred_element_type=F32)

    @pl.loop(0, GRID // 256)
    def _(i):
        at = pl.ds(pl.multiple_of(i * 256, 256), 256)
        hi, lo = hi_ref[at], lo_ref[at]
        y = dot(rl[...], hi) + dot(rh[...], lo) + dot(rh[...], hi)
        o_ref[:, :, at] = s_ref[:, :, at] * y.reshape(CH, ROWS, 256)


def mix_columns(hi, lo, r, sigma):
    return pl.pallas_call(
        columns_kernel,
        out_shape=jax.ShapeDtypeStruct((CH, ROWS, GRID), F32),
        in_specs=[VMEM] * 4,
        out_specs=VMEM,
        scratch_shapes=[pltpu.VMEM((CH * ROWS, GRID), BF16)] * 2,
        compiler_params=params(4),
        name="mix_columns",
    )(hi, lo, r, sigma)


def to_next_window(ends):
    windows = lax.axis_size("tm")
    last = range(PLANES - 1, windows - 1, PLANES)
    along = [(i, i + 1) for i in range(windows - 1) if (i + 1) % PLANES]
    quarters = [pair for _, *pairs in ends for pair in pairs]
    arrived, relayed = [], []
    for half, *_ in ends:
        arrived.append(lax.ppermute(half, "tm", along))
    for plane, quarter in zip((0, 2, 1, PLANES - 1), quarters):
        if plane != PLANES - 1:
            quarter = lax.ppermute(quarter, "tm", [(w, w + 1 - PLANES + plane) for w in last])
        relayed.append(lax.ppermute(quarter, "tm", [(w + 1 - PLANES + plane, w + 1) for w in last]))
    return arrived + relayed


def gather_correlation(correlation):
    own = lax.all_to_all(deal(correlation), "band", 0, 0, tiled=True)
    far, near = BANDS // 2, 1
    beside = lax.ppermute(own, "band", [(b, b ^ far) for b in range(BANDS)])
    across = lax.ppermute(own, "band", [(b, b ^ near) for b in range(BANDS)])
    return own, beside, across, lax.ppermute(beside, "band", [(b, b ^ near) for b in range(BANDS)])


def defects(increments, velocity, diffusivity, scaling, correlation):
    x = increments.reshape(CH, ROWS, GRID)
    v = velocity[0]
    sigma = scaling.reshape(CH, ROWS, GRID)
    up = [(i, i + 1) for i in range(BANDS - 1)]
    down = [(j, i) for i, j in up]
    lo_edge, hi_edge = pack_edges(x, v)
    before = lax.ppermute(hi_edge, "band", up)
    after = lax.ppermute(lo_edge, "band", down)
    band = lax.axis_index("band").reshape(1)
    diffuse = diffusivity.reshape(CH)
    ends = []
    for base in (0, CH // 2):
        ends.append(propagate(base, x, v, before, after, diffuse, band))
    sent = combine(x, to_next_window(ends), sigma)
    blocks = gather_correlation(correlation)
    mine = lax.all_to_all(sent, "band", 0, 0, tiled=True)
    mixed, hi, lo = mix_rows(quarter_of(band), blocks, mine)
    back = lax.all_to_all(mixed, "band", 0, 0, tiled=True)
    return mix_columns(hi, lo, back, sigma).reshape(1, FIELDS, LEVELS, ROWS, GRID)


def solution(mesh):
    return jax.shard_map(
        defects,
        mesh=mesh,
        in_specs=(
            P("tm", None, None, "band", None),
            P("tm", None, "band", None),
            P(),
            P(None, None, "band", None),
            P("band", None),
        ),
        out_specs=P("tm", None, None, "band", None),
        check_vma=False,
    )
```

```python
import functools

import jax
import jax.numpy as jnp
from jax import lax
from jax.experimental import pallas as pl
from jax.experimental.pallas import tpu as pltpu
from jax.sharding import PartitionSpec as P


FIELDS = 4
LEVELS = 2
STEPS = 4
CH = FIELDS * LEVELS
ROWS = 32
GRID = 1024
BANDS = 32
QUARTERS = BANDS // CH
COLS = GRID // QUARTERS
PLANES = 4
F32 = jnp.float32
BF16 = jnp.bfloat16


def in_hbm(*arrays):
    return [pltpu.with_memory_space_constraint(a, pltpu.HBM) for a in arrays]


def start_all(pairs, sem):
    copies = [pltpu.make_async_copy(src, dst, sem.at[i]) for i, (src, dst) in enumerate(pairs)]
    for copy in copies:
        copy.start()
    return copies


def params(mib):
    return pltpu.CompilerParams(vmem_limit_bytes=mib << 20)


VMEM = pl.BlockSpec(memory_space=pltpu.VMEM)
SMEM = pl.BlockSpec(memory_space=pltpu.SMEM)
HBM = pl.BlockSpec(memory_space=pltpu.HBM)
EDGE = jax.ShapeDtypeStruct((CH // 2 + 1, 8, GRID), F32)


def pack_kernel(x_hbm, v_hbm, lo_ref, hi_ref, xe, ve, sem):
    pairs = [
        (src.at[:, at : at + 8], dst.at[j]) for src, dst in ((x_hbm, xe), (v_hbm, ve)) for j, at in enumerate((0, ROWS - 8))
    ]
    for copy in start_all(pairs, sem):
        copy.wait()
    row = lax.broadcasted_iota(jnp.int32, (8, GRID), 0)
    for k in range(CH // 2 + 1):
        ref, at = (xe, 2 * k) if k < CH // 2 else (ve, 0)
        lo_ref[k] = jnp.where(row < 4, ref[0, at], pltpu.roll(ref[0, at + 1], 4, 0))
        hi_ref[k] = jnp.where(row < 4, pltpu.roll(ref[1, at], 4, 0), ref[1, at + 1])


def pack_edges(x, v):
    return pl.pallas_call(
        pack_kernel,
        out_shape=(EDGE, EDGE),
        in_specs=[HBM, HBM],
        out_specs=(VMEM, VMEM),
        scratch_shapes=[
            pltpu.VMEM((2, CH, 8, GRID), F32),
            pltpu.VMEM((2, 2, 8, GRID), F32),
            pltpu.SemaphoreType.DMA((4,)),
        ],
        compiler_params=params(3),
        name="pack_edges",
    )(*in_hbm(x, v))


def stencil_kernel(base, k_ref, band_ref, x_ref, v_ref, before_ref, after_ref, o_ref, first, second, buf, vel):
    row = lax.broadcasted_iota(jnp.int32, (8, GRID), 0)

    def edge(above, below, odd):
        swap = lambda t: pltpu.roll(t, 4, 0)
        pick = lambda a, b: jnp.where(row < 4, b, a)
        return pick(above, swap(below)) if odd else pick(swap(above), below)

    for d in range(2):
        vel[d, 0:8] = 0.5 * edge(before_ref[CH // 2], after_ref[CH // 2], d)
        vel[d, 8:40] = 0.5 * v_ref[d]
    band = band_ref[0]
    within = jnp.where(row < 4, (band < BANDS - 1).astype(F32), (band > 0).astype(F32))

    def field(pair, odd):
        c = 2 * pair + odd
        pairs_ref = (first, second)[pair]
        k = k_ref[base + c]
        outer = k * within
        fringe = edge(before_ref[base // 2 + pair], after_ref[base // 2 + pair], odd)
        buf[0, 0:8] = fringe
        buf[0, 8:40] = x_ref[base + c]
        buf[0, 40:48] = fringe
        for s in range(STEPS):
            src, dst = s % 2, (s + 1) % 2
            last = s == STEPS - 1
            for t in range(1 if last else 0, 5):
                r = 8 * t
                kk = k if t else outer
                x = buf[src, r : r + 8]
                up = buf[src, r + 1 : r + 9]
                lo = buf[src, r - 1 : r + 7] if t else buf[src, 39:47]
                e = pltpu.roll(x, GRID - 1, 1)
                w = pltpu.roll(x, 1, 1)
                y = x - vel[0, r : r + 8] * (e - w) - vel[1, r : r + 8] * (up - lo)
                y = y + kk * (up + lo + e + w - 4.0 * x)
                if last:
                    o_ref[c, r - 8 : r] = y
                    pairs_ref[odd, r - 8 : r] = y
                else:
                    buf[dst, r : r + 8] = y
                    if t == 0:
                        buf[dst, 40:48] = y

    for pair in range(2):
        field(pair, 0)
        field(pair, 1)


def propagate(base, x, v, before, after, diffuse, band):
    return pl.pallas_call(
        functools.partial(stencil_kernel, base),
        out_shape=tuple(jax.ShapeDtypeStruct((n, ROWS, GRID), F32) for n in (4, 2, 2)),
        in_specs=[SMEM, SMEM, VMEM, VMEM, VMEM, VMEM],
        out_specs=(VMEM, VMEM, VMEM),
        scratch_shapes=[pltpu.VMEM((2, 48, GRID), F32), pltpu.VMEM((2, 40, GRID), F32)],
        compiler_params=params(2),
        name="propagate",
    )(diffuse, band, x, v, before, after)


def combine_kernel(x_ref, along0, along1, p0, p1, p2, p3, s_ref, o_hbm, buf, sem):
    half = CH // 2
    copies = []
    for c in range(CH):
        arrived = (along0 if c < half else along1)[c % half] + (p0, p1, p2, p3)[c // 2][c % 2]
        y = s_ref[c] * (x_ref[c] - arrived)
        at = slice(c * QUARTERS, (c + 1) * QUARTERS)
        for q in range(QUARTERS):
            buf[c * QUARTERS + q] = y[:, q * COLS : (q + 1) * COLS]
        copy = pltpu.make_async_copy(buf.at[at], o_hbm.at[at], sem.at[c])
        copy.start()
        copies.append(copy)
    for copy in copies:
        copy.wait()


def combine(x, arrived, sigma):
    return pl.pallas_call(
        combine_kernel,
        out_shape=jax.ShapeDtypeStruct((BANDS, ROWS, COLS), F32),
        in_specs=[VMEM] * 8,
        out_specs=HBM,
        scratch_shapes=[pltpu.VMEM((BANDS, ROWS, COLS), F32), pltpu.SemaphoreType.DMA((CH,))],
        compiler_params=params(3),
        name="combine",
    )(x, *arrived, sigma)


def halves(x):
    hi = x.astype(BF16)
    return hi, (x - hi.astype(F32)).astype(BF16)


def rows_kernel(c_ref, x_ref, o_ref, hi_ref, lo_ref, xh, xl):
    @pl.when(pl.program_id(0) == 0)
    def _():
        xh[...], xl[...] = halves(x_ref[...].reshape(GRID, COLS))

    hi_ref[...], lo_ref[...] = halves(c_ref[...])
    dot = lambda a, b: jnp.dot(a, b, preferred_element_type=F32)
    y = dot(hi_ref[...], xl[...]) + dot(lo_ref[...], xh[...]) + dot(hi_ref[...], xh[...])
    o_ref[...] = y.reshape(8, ROWS, COLS)


def mix_rows(c, x):
    whole = pl.BlockSpec((256, GRID), lambda i: (i, 0))
    shape = jax.ShapeDtypeStruct((GRID, GRID), BF16)
    return pl.pallas_call(
        rows_kernel,
        grid=(GRID // 256,),
        out_shape=(jax.ShapeDtypeStruct((BANDS, ROWS, COLS), F32), shape, shape),
        in_specs=[whole, pl.BlockSpec((BANDS, ROWS, COLS), lambda i: (0, 0, 0))],
        out_specs=(pl.BlockSpec((8, ROWS, COLS), lambda i: (i, 0, 0)), whole, whole),
        scratch_shapes=[pltpu.VMEM((GRID, COLS), BF16)] * 2,
        compiler_params=params(12),
        name="mix_rows",
    )(*in_hbm(c), x)


def columns_kernel(hi_ref, lo_ref, r_ref, s_ref, o_hbm, rh, rl, buf, sem):
    for c in range(CH):
        for q in range(QUARTERS):
            at = slice(c * ROWS, (c + 1) * ROWS), slice(q * COLS, (q + 1) * COLS)
            rh[at], rl[at] = halves(r_ref[c * QUARTERS + q])

    dot = lambda a, b: lax.dot_general(a, b, (((1,), (1,)), ((), ())), preferred_element_type=F32)

    copies = []
    for i in range(GRID // 256):
        at = slice(i * 256, (i + 1) * 256)
        hi, lo = hi_ref[at], lo_ref[at]
        y = dot(rl[...], hi) + dot(rh[...], lo) + dot(rh[...], hi)
        buf[:, :, at] = s_ref[:, :, at] * y.reshape(CH, ROWS, 256)
        copies.append(pltpu.make_async_copy(buf.at[:, :, at], o_hbm.at[:, :, at], sem.at[i]))
        copies[i].start()
    for copy in copies:
        copy.wait()


def mix_columns(hi, lo, r, sigma):
    return pl.pallas_call(
        columns_kernel,
        out_shape=jax.ShapeDtypeStruct((CH, ROWS, GRID), F32),
        in_specs=[VMEM] * 4,
        out_specs=HBM,
        scratch_shapes=[pltpu.VMEM((CH * ROWS, GRID), BF16)] * 2
        + [pltpu.VMEM((CH, ROWS, GRID), F32), pltpu.SemaphoreType.DMA((GRID // 256,))],
        compiler_params=params(5),
        name="mix_columns",
    )(hi, lo, r, sigma)


def to_next_window(ends):
    windows = lax.axis_size("tm")
    last = range(PLANES - 1, windows - 1, PLANES)
    along = [(i, i + 1) for i in range(windows - 1) if (i + 1) % PLANES]
    quarters = [pair for _, *pairs in ends for pair in pairs]
    arrived, relayed = [], []
    for half, *_ in ends:
        arrived.append(lax.ppermute(half, "tm", along))
    for plane, quarter in zip((0, PLANES - 1, 1, PLANES - 1), quarters):
        if plane != PLANES - 1:
            quarter = lax.ppermute(quarter, "tm", [(w, w + 1 - PLANES + plane) for w in last])
        relayed.append(lax.ppermute(quarter, "tm", [(w + 1 - PLANES + plane, w + 1) for w in last]))
    return arrived + relayed


def defects(increments, velocity, diffusivity, scaling, correlation):
    x = increments.reshape(CH, ROWS, GRID)
    v = velocity[0]
    sigma = scaling.reshape(CH, ROWS, GRID)
    up = [(i, i + 1) for i in range(BANDS - 1)]
    down = [(j, i) for i, j in up]
    lo_edge, hi_edge = pack_edges(x, v)
    before = lax.ppermute(hi_edge, "band", up)
    after = lax.ppermute(lo_edge, "band", down)
    band = lax.axis_index("band").reshape(1)
    diffuse = diffusivity.reshape(CH)
    ends = []
    for base in (0, CH // 2):
        ends.append(propagate(base, x, v, before, after, diffuse, band))
    sent = combine(x, to_next_window(ends), sigma)
    full = lax.all_gather(correlation, "band", axis=0, tiled=True)
    mine = lax.all_to_all(sent, "band", 0, 0, tiled=True)
    mixed, hi, lo = mix_rows(full, mine)
    back = lax.all_to_all(mixed, "band", 0, 0, tiled=True)
    return mix_columns(hi, lo, back, sigma).reshape(1, FIELDS, LEVELS, ROWS, GRID)


def solution(mesh):
    return jax.shard_map(
        defects,
        mesh=mesh,
        in_specs=(
            P("tm", None, None, "band", None),
            P("tm", None, "band", None),
            P(),
            P(None, None, "band", None),
            P("band", None),
        ),
        out_specs=P("tm", None, None, "band", None),
        check_vma=False,
    )
```

```python
import functools

import jax
import jax.numpy as jnp
from jax import lax
from jax.experimental import pallas as pl
from jax.experimental.pallas import tpu as pltpu
from jax.sharding import PartitionSpec as P


FIELDS = 4
LEVELS = 2
STEPS = 4
CH = FIELDS * LEVELS
ROWS = 32
GRID = 1024
BANDS = 32
QUARTERS = BANDS // CH
COLS = GRID // QUARTERS
PLANES = 4
F32 = jnp.float32
BF16 = jnp.bfloat16


def in_hbm(*arrays):
    return [pltpu.with_memory_space_constraint(a, pltpu.HBM) for a in arrays]


def start_all(pairs, sem):
    copies = [pltpu.make_async_copy(src, dst, sem.at[i]) for i, (src, dst) in enumerate(pairs)]
    for copy in copies:
        copy.start()
    return copies


def params(mib):
    return pltpu.CompilerParams(vmem_limit_bytes=mib << 20)


VMEM = pl.BlockSpec(memory_space=pltpu.VMEM)
SMEM = pl.BlockSpec(memory_space=pltpu.SMEM)
HBM = pl.BlockSpec(memory_space=pltpu.HBM)
EDGE = jax.ShapeDtypeStruct((CH // 2 + 1, 8, GRID), F32)


def pack_kernel(x_hbm, v_hbm, lo_ref, hi_ref, xe, ve, sem):
    pairs = [
        (src.at[:, at : at + 8], dst.at[j]) for src, dst in ((x_hbm, xe), (v_hbm, ve)) for j, at in enumerate((0, ROWS - 8))
    ]
    for copy in start_all(pairs, sem):
        copy.wait()
    row = lax.broadcasted_iota(jnp.int32, (8, GRID), 0)
    for k in range(CH // 2 + 1):
        ref, at = (xe, 2 * k) if k < CH // 2 else (ve, 0)
        lo_ref[k] = jnp.where(row < 4, ref[0, at], pltpu.roll(ref[0, at + 1], 4, 0))
        hi_ref[k] = jnp.where(row < 4, pltpu.roll(ref[1, at], 4, 0), ref[1, at + 1])


def pack_edges(x, v):
    return pl.pallas_call(
        pack_kernel,
        out_shape=(EDGE, EDGE),
        in_specs=[HBM, HBM],
        out_specs=(VMEM, VMEM),
        scratch_shapes=[
            pltpu.VMEM((2, CH, 8, GRID), F32),
            pltpu.VMEM((2, 2, 8, GRID), F32),
            pltpu.SemaphoreType.DMA((4,)),
        ],
        compiler_params=params(3),
        name="pack_edges",
    )(*in_hbm(x, v))


def stencil_kernel(base, k_ref, band_ref, x_ref, v_ref, before_ref, after_ref, o_ref, first, second, buf, vel):
    row = lax.broadcasted_iota(jnp.int32, (8, GRID), 0)

    def edge(above, below, odd):
        swap = lambda t: pltpu.roll(t, 4, 0)
        pick = lambda a, b: jnp.where(row < 4, b, a)
        return pick(above, swap(below)) if odd else pick(swap(above), below)

    for d in range(2):
        vel[d, 0:8] = 0.5 * edge(before_ref[CH // 2], after_ref[CH // 2], d)
        vel[d, 8:40] = 0.5 * v_ref[d]
    band = band_ref[0]
    within = jnp.where(row < 4, (band < BANDS - 1).astype(F32), (band > 0).astype(F32))

    def field(pair, odd):
        c = 2 * pair + odd
        pairs_ref = (first, second)[pair]
        k = k_ref[base + c]
        outer = k * within
        fringe = edge(before_ref[base // 2 + pair], after_ref[base // 2 + pair], odd)
        buf[0, 0:8] = fringe
        buf[0, 8:40] = x_ref[base + c]
        buf[0, 40:48] = fringe
        for s in range(STEPS):
            src, dst = s % 2, (s + 1) % 2
            last = s == STEPS - 1
            for t in range(1 if last else 0, 5):
                r = 8 * t
                kk = k if t else outer
                x = buf[src, r : r + 8]
                up = buf[src, r + 1 : r + 9]
                lo = buf[src, r - 1 : r + 7] if t else buf[src, 39:47]
                e = pltpu.roll(x, GRID - 1, 1)
                w = pltpu.roll(x, 1, 1)
                y = x - vel[0, r : r + 8] * (e - w) - vel[1, r : r + 8] * (up - lo)
                y = y + kk * (up + lo + e + w - 4.0 * x)
                if last:
                    o_ref[c, r - 8 : r] = y
                    pairs_ref[odd, r - 8 : r] = y
                else:
                    buf[dst, r : r + 8] = y
                    if t == 0:
                        buf[dst, 40:48] = y

    for pair in range(2):
        field(pair, 0)
        field(pair, 1)


def propagate(base, x, v, before, after, diffuse, band):
    return pl.pallas_call(
        functools.partial(stencil_kernel, base),
        out_shape=tuple(jax.ShapeDtypeStruct((n, ROWS, GRID), F32) for n in (4, 2, 2)),
        in_specs=[SMEM, SMEM, VMEM, VMEM, VMEM, VMEM],
        out_specs=(VMEM, VMEM, VMEM),
        scratch_shapes=[pltpu.VMEM((2, 48, GRID), F32), pltpu.VMEM((2, 40, GRID), F32)],
        compiler_params=params(2),
        name="propagate",
    )(diffuse, band, x, v, before, after)


def combine_kernel(x_ref, along0, along1, p0, p1, p2, p3, s_ref, o_hbm, buf, sem):
    half = CH // 2
    copies = []
    for c in range(CH):
        arrived = (along0 if c < half else along1)[c % half] + (p0, p1, p2, p3)[c // 2][c % 2]
        y = s_ref[c] * (x_ref[c] - arrived)
        at = slice(c * QUARTERS, (c + 1) * QUARTERS)
        for q in range(QUARTERS):
            buf[c * QUARTERS + q] = y[:, q * COLS : (q + 1) * COLS]
        copy = pltpu.make_async_copy(buf.at[at], o_hbm.at[at], sem.at[c])
        copy.start()
        copies.append(copy)
    for copy in copies:
        copy.wait()


def combine(x, arrived, sigma):
    return pl.pallas_call(
        combine_kernel,
        out_shape=jax.ShapeDtypeStruct((BANDS, ROWS, COLS), F32),
        in_specs=[VMEM] * 8,
        out_specs=HBM,
        scratch_shapes=[pltpu.VMEM((BANDS, ROWS, COLS), F32), pltpu.SemaphoreType.DMA((CH,))],
        compiler_params=params(3),
        name="combine",
    )(x, *arrived, sigma)


def halves(x):
    hi = x.astype(BF16)
    return hi, (x - hi.astype(F32)).astype(BF16)


def rows_kernel(c_ref, x_ref, o_ref, xh, xl):
    @pl.when(pl.program_id(0) == 0)
    def _():
        xh[...], xl[...] = halves(x_ref[...].reshape(GRID, COLS))

    hi, lo = halves(c_ref[...])
    dot = lambda a, b: jnp.dot(a, b, preferred_element_type=F32)
    y = dot(hi, xl[...]) + dot(lo, xh[...]) + dot(hi, xh[...])
    o_ref[...] = y.reshape(8, ROWS, COLS)


def mix_rows(c, x):
    whole = pl.BlockSpec((256, GRID), lambda i: (i, 0))
    return pl.pallas_call(
        rows_kernel,
        grid=(GRID // 256,),
        out_shape=jax.ShapeDtypeStruct((BANDS, ROWS, COLS), F32),
        in_specs=[whole, pl.BlockSpec((BANDS, ROWS, COLS), lambda i: (0, 0, 0))],
        out_specs=pl.BlockSpec((8, ROWS, COLS), lambda i: (i, 0, 0)),
        scratch_shapes=[pltpu.VMEM((GRID, COLS), BF16)] * 2,
        compiler_params=params(12),
        name="mix_rows",
    )(*in_hbm(c), x)


def columns_kernel(c_ref, r_ref, s_ref, o_hbm, rh, rl, buf, sem):
    for c in range(CH):
        for q in range(QUARTERS):
            at = slice(c * ROWS, (c + 1) * ROWS), slice(q * COLS, (q + 1) * COLS)
            rh[at], rl[at] = halves(r_ref[c * QUARTERS + q])

    dot = lambda a, b: lax.dot_general(a, b, (((1,), (1,)), ((), ())), preferred_element_type=F32)

    copies = []
    for i in range(GRID // 256):
        at = slice(i * 256, (i + 1) * 256)
        hi, lo = halves(c_ref[at])
        y = dot(rl[...], hi) + dot(rh[...], lo) + dot(rh[...], hi)
        buf[:, :, at] = s_ref[:, :, at] * y.reshape(CH, ROWS, 256)
        copies.append(pltpu.make_async_copy(buf.at[:, :, at], o_hbm.at[:, :, at], sem.at[i]))
        copies[i].start()
    for copy in copies:
        copy.wait()


def mix_columns(c, r, sigma):
    return pl.pallas_call(
        columns_kernel,
        out_shape=jax.ShapeDtypeStruct((CH, ROWS, GRID), F32),
        in_specs=[VMEM] * 3,
        out_specs=HBM,
        scratch_shapes=[pltpu.VMEM((CH * ROWS, GRID), BF16)] * 2
        + [pltpu.VMEM((CH, ROWS, GRID), F32), pltpu.SemaphoreType.DMA((GRID // 256,))],
        compiler_params=params(8),
        name="mix_columns",
    )(c, r, sigma)


def to_next_window(ends):
    windows = lax.axis_size("tm")
    last = range(PLANES - 1, windows - 1, PLANES)
    along = [(i, i + 1) for i in range(windows - 1) if (i + 1) % PLANES]
    quarters = [pair for _, *pairs in ends for pair in pairs]
    arrived, relayed = [], []
    for half, *_ in ends:
        arrived.append(lax.ppermute(half, "tm", along))
    for plane, quarter in zip((0, PLANES - 1, 1, PLANES - 1), quarters):
        if plane != PLANES - 1:
            quarter = lax.ppermute(quarter, "tm", [(w, w + 1 - PLANES + plane) for w in last])
        relayed.append(lax.ppermute(quarter, "tm", [(w + 1 - PLANES + plane, w + 1) for w in last]))
    return arrived + relayed


def defects(increments, velocity, diffusivity, scaling, correlation):
    x = increments.reshape(CH, ROWS, GRID)
    v = velocity[0]
    sigma = scaling.reshape(CH, ROWS, GRID)
    up = [(i, i + 1) for i in range(BANDS - 1)]
    down = [(j, i) for i, j in up]
    lo_edge, hi_edge = pack_edges(x, v)
    before = lax.ppermute(hi_edge, "band", up)
    after = lax.ppermute(lo_edge, "band", down)
    band = lax.axis_index("band").reshape(1)
    diffuse = diffusivity.reshape(CH)
    ends = []
    for base in (0, CH // 2):
        ends.append(propagate(base, x, v, before, after, diffuse, band))
    sent = combine(x, to_next_window(ends), sigma)
    full = lax.all_gather(correlation, "band", axis=0, tiled=True)
    mine = lax.all_to_all(sent, "band", 0, 0, tiled=True)
    mixed = mix_rows(full, mine)
    back = lax.all_to_all(mixed, "band", 0, 0, tiled=True)
    return mix_columns(full, back, sigma).reshape(1, FIELDS, LEVELS, ROWS, GRID)


def solution(mesh):
    return jax.shard_map(
        defects,
        mesh=mesh,
        in_specs=(
            P("tm", None, None, "band", None),
            P("tm", None, "band", None),
            P(),
            P(None, None, "band", None),
            P("band", None),
        ),
        out_specs=P("tm", None, None, "band", None),
        check_vma=False,
    )
```
